32 devices in a mesh: groups: 2 (over x), tensor: 16 (over z, y, core).
Axes of the slice: x: 2, y: 2, z: 4, core: 2. Of those that a mesh axis runs over, the one named last changes fastest.
Arguments:
- queries: bfloat16 [256, 4096], P(('groups', 'tensor')), parts along dimension 0, may hold values from -6 to 6
- corpus: bfloat16 [2048, 4, 4096], P(('groups', 'tensor')), parts along dimension 0, may hold values from -6 to 6
- block_owner: int32 [48, 1], P('groups'), parts along dimension 0, may hold values from 0 to 15; in each aligned block of 24 rows (0 to 23, 24 to 47, ...) at most 3 rows name the same one
- slot_row: int32 [48], P('groups'), parts along dimension 0, may hold values from 0 to 63
- segment: int32 [48], P('groups'), parts along dimension 0, may hold values from 0 to 3, never falling along the last dimension, each value on 1 to 12 neighbouring positions
- query_weight: bfloat16 [1024, 4096], P('tensor'), may hold values from -3 to 3
- key_weight: bfloat16 [1024, 4096], P('tensor'), may hold values from -3 to 3
- value_weight: bfloat16 [1024, 4096], P('tensor'), may hold values from -0.09375 to 0.09375
- out_weight: bfloat16 [1024, 4096], P('tensor'), may hold values from -0.1875 to 0.1875
- gain_attn: float32 [4096], replicated, may hold values from 0.1 to 1.9
- gain_ffn: float32 [4096], replicated, may hold values from 0.1 to 1.9
- gate_weight: bfloat16 [2560, 4096], P('tensor'), may hold values from -0.09375 to 0.09375
- up_weight: bfloat16 [2560, 4096], P('tensor'), may hold values from -0.09375 to 0.09375
- down_weight: bfloat16 [2560, 4096], P('tensor'), may hold values from -0.125 to 0.125
Outputs:
- encoded: bfloat16 [448, 4096], P(('groups', 'tensor')), parts along dimension 0
The draws below stay inside these ranges and needn't reach their ends.
There are 2 independent parts, one for each index of `groups`. The reference program is written for one: setup_inputs(seed, part) draws one part's arguments, and reference() takes and returns one part's arrays. A program takes and returns all parts, laid end to end along the dimension named above; an argument that names none is the same for every part. Nothing has to cross between parts.
Inputs may be any that keep to these rules, and one draw needn't show every extreme that they name: `block_owner`: every owner holds some block of the pack; no owner holds more than 3 of them, and some owner holds exactly 3. `segment`: never falls along the pack; each pair has 1 to 12 blocks, one exactly 12.
All inputs are finite; a program needn't handle non-finite values.
Results may differ from the reference program's by a relative error of at most 0.008.
Values may be sent and summed in bfloat16 or wider, within the bound.
A program may use at most 64 MiB of HBM per device.

```python
import math
import jax
import jax.numpy as jnp
import numpy as np
from jax import lax

D = 4096
HDIM = 64
QLEN = 32
PAIRS = 4
BLK = 4
CAP = 3
CORP_DEV = 64
HEADS = 16
FF = 2560
NBLK = 24
MOSTB = 12
QROWS = 128
TOK = 224
CORPUS = 1024
N_TENSOR = 16


def shared_base(key):
    return jax.random.truncated_normal(jax.random.fold_in(key, 11), -4.0, 4.0, (HEADS * HDIM, D), jnp.float32) * D ** (-0.5)


def draw_query_weight(key, part):
    base_matrix = shared_base(key)
    return base_matrix.astype(jnp.bfloat16)


def draw_key_weight(key, part):
    other_matrix = jax.random.truncated_normal(jax.random.fold_in(key, 23), -4.0, 4.0, (HEADS * HDIM, D), jnp.float32) * D ** (-0.5)
    return other_matrix.astype(jnp.bfloat16)


def touch_ends(result, own_key, low, largest):
    spot = [jax.random.randint(jax.random.fold_in(own_key, axis), (), 0, length) for axis, length in enumerate(result.shape)]
    longest = result.shape.index(max(result.shape))
    next_to = spot[:longest] + [(spot[longest] + 1) % result.shape[longest]] + spot[longest + 1:]
    return result.at[tuple(spot)].set(low).at[tuple(next_to)].set(largest)


def block_scale(rng, extent, cuts, least, top_value):
    def one(position, shards_of):
        draws = jax.random.uniform(jax.random.fold_in(jax.random.fold_in(rng, 6), position), (shards_of,), jnp.float32, least / len(cuts), top_value / len(cuts))
        return jnp.repeat(jnp.exp(draws), extent[position] // shards_of).reshape((-1,) + (1,) * (len(extent) - position - 1))

    level = one(*cuts[0])
    for cut in cuts[1:]:
        level = level * one(*cut)
    return level


def length_profile(amount, total, limit, lean):
    loads = [(1 << 20) // math.isqrt(standing ** lean) + 1 for standing in range(2, amount + 1)]
    surplus, counts = total - limit - (amount - 1), [1] * (amount - 1)
    while surplus > 0:
        movable = [i for i in range(amount - 1) if counts[i] < limit]
        pool, left = sum([loads[i] for i in movable]), surplus
        for i in movable:
            extra = min(limit - counts[i], max(1, left * loads[i] // pool), surplus)
            counts[i] = counts[i] + extra
            surplus = surplus - extra
    return np.array([limit] + counts)


def ragged_sizes(stream_key, count, total, limit, skew):
    if count == 2:
        one = jax.random.randint(stream_key, (), max(1, total - limit), min(limit, total - 1) + 1)
        return jnp.stack([one, total - one])
    sizes = jnp.asarray(length_profile(count, total, limit, skew), jnp.int32)
    couples = (count - 1) // 2
    donor, sink = sizes[1:1 + 2 * couples:2], sizes[2:2 + 2 * couples:2]
    slack = jnp.minimum(donor - 1, limit - sink)
    passed = jax.random.randint(jax.random.fold_in(stream_key, 1), (couples,), 0, 1 << 20) % (slack + 1)
    sizes = sizes.at[1:1 + 2 * couples:2].set(donor - passed).at[2:2 + 2 * couples:2].set(sink + passed)
    return sizes[jax.random.permutation(jax.random.fold_in(stream_key, 2), count)]


def shared_out(rng, own, number, rows, count, top, bound, slope):
    order = jax.random.permutation(rng, count)
    heavy_load, ordinary = portions_of(count, rows * top, bound, slope, True), portions_of(count, rows * top, bound, slope, False)
    places = jnp.arange(count)

    def named(tallies, turn):
        used = int((tallies > 0).sum())
        fixed = max(1, used // 4)
        moved = fixed + (places - fixed + turn * (used - fixed)) % max(1, count - fixed)
        return jnp.zeros((count,), jnp.int32).at[order[jnp.where(places < fixed, places, moved)]].set(jnp.asarray(tallies, jnp.int32))

    tallies = jnp.where(number % 4 == 0, named(heavy_load, number // 4), named(ordinary, number - number // 4 - 1))
    mixed = jax.random.permutation(jax.random.fold_in(own, 3), count)
    giver, taker = mixed[0:count // 2 * 2:2], mixed[1:count // 2 * 2:2]
    margin = jnp.minimum(tallies[giver] - 1, bound - tallies[taker]) // 2
    margin = jnp.where((giver == order[0]) | (taker == order[0]) | (tallies[taker] == 0), 0, jnp.maximum(margin, 0))
    moved = jax.random.randint(jax.random.fold_in(own, 4), (count // 2,), 0, 1 << 20) % (margin + 1)
    tallies = tallies.at[giver].add(-moved).at[taker].add(moved)
    labels = jnp.searchsorted(jnp.cumsum(tallies), jnp.arange(rows * top), side="right").astype(jnp.int32)
    grid = labels.reshape(top, rows).T
    grid = grid[jax.random.permutation(jax.random.fold_in(own, 1), rows)]
    turn = jax.random.randint(jax.random.fold_in(own, 2), (rows, 1), 0, top)
    return jnp.take_along_axis(grid, (jnp.arange(top)[None, :] + turn) % top, axis=1)


def portions_of(amount, total, reach, slope, full):
    loads = [(1 << 20) // math.isqrt(standing ** slope) + 1 for standing in range(1, amount + 1)]
    largest = reach if full else min(reach, max(-(-total // amount), total * loads[0] // sum(loads)))
    least = 1 if total - largest >= amount - 1 else 0
    holding, surplus = [largest] + [least] * (amount - 1), total - largest - least * (amount - 1)
    while surplus > 0:
        candidates = [i for i in range(1, amount) if holding[i] < largest] or [i for i in range(1, amount) if holding[i] < reach]
        whole, left = sum([loads[i] for i in candidates]), surplus
        for i in candidates:
            more = min(reach - holding[i], max(1, left * loads[i] // whole), surplus)
            holding[i] = holding[i] + more
            surplus = surplus - more
    return np.array(holding)


def gaussian(rng, dims, spread, reach, pieces=(), held_as=jnp.bfloat16):
    level = block_scale(rng, dims, pieces, -0.22, 0.18) if pieces else 1.0
    values = jax.random.normal(rng, dims, jnp.float32) * spread * level
    return jnp.minimum(jnp.maximum(values, -reach), reach).astype(held_as)


def setup_inputs(seed: int = 0, part: int = 0) -> dict:
    streams_of = jax.random.split(jax.random.key(seed), 15)
    part_keys = jax.random.split(jax.random.fold_in(streams_of[14], part), 15)
    queries = gaussian(part_keys[0], (QROWS, D), 1.0, 6.0, ((0, 16),))
    corpus = gaussian(part_keys[1], (CORPUS, BLK, D), 1.0, 6.0, ((0, 16),))
    block_owner_keys = jax.random.split(jax.random.fold_in(part_keys[2], 1), NBLK // NBLK)
    block_owner_turns = jax.random.permutation(jax.random.fold_in(part_keys[2], 3), NBLK // NBLK)
    block_owner = jax.vmap(lambda own, number: shared_out(jax.random.fold_in(part_keys[2], 2), own, number, NBLK, N_TENSOR, 1, CAP, 2))(block_owner_keys, block_owner_turns).reshape((NBLK, 1))
    slot_row = touch_ends(jax.random.randint(part_keys[3], (NBLK,), 0, CORP_DEV), jax.random.fold_in(part_keys[3], 1), 0, CORP_DEV - 1).astype(jnp.int32)
    segment = jnp.searchsorted(jnp.cumsum(ragged_sizes(part_keys[4], PAIRS, NBLK, MOSTB, 1)), jnp.arange(NBLK), side="right").astype(jnp.int32)
    query_weight = draw_query_weight(jax.random.fold_in(streams_of[14], 71), part)
    key_weight = draw_key_weight(jax.random.fold_in(streams_of[14], 71), part)
    value_weight = gaussian(streams_of[7], (HEADS * HDIM, D), D ** -0.5, 0.09375, ((0, 16),))
    out_weight = gaussian(streams_of[8], (HEADS * HDIM, D), (HEADS * HDIM) ** -0.5, 0.1875, ((0, 16),))
    gain_attn = jnp.clip(1.0 + 0.18 * jax.random.normal(streams_of[9], (D,), jnp.float32), 0.1, 1.9)
    gain_ffn = jnp.clip(1.0 + 0.18 * jax.random.normal(streams_of[10], (D,), jnp.float32), 0.1, 1.9)
    gate_weight = gaussian(streams_of[11], (FF, D), D ** -0.5, 0.09375, ((0, 16),))
    up_weight = gaussian(streams_of[12], (FF, D), D ** -0.5, 0.09375, ((0, 16),))
    down_weight = gaussian(streams_of[13], (FF, D), FF ** -0.5, 0.125, ((0, 16),))
    return dict(queries=queries, corpus=corpus, block_owner=block_owner, slot_row=slot_row, segment=segment, query_weight=query_weight, key_weight=key_weight, value_weight=value_weight, out_weight=out_weight, gain_attn=gain_attn, gain_ffn=gain_ffn, gate_weight=gate_weight, up_weight=up_weight, down_weight=down_weight)


def normed(stream, gain):
    values = stream.astype(jnp.float32)
    mean_square = lax.optimization_barrier(jnp.mean(values * values, axis=-1, keepdims=True))
    return (values * lax.rsqrt(mean_square + 1e-06) * gain).astype(jnp.bfloat16)

def by_rows(left, weight):
    return lax.dot_general(left, weight, (((1,), (1,)), ((), ())), preferred_element_type=jnp.float32)

def reference(queries, corpus, block_owner, slot_row, segment, query_weight, key_weight, value_weight, out_weight, gain_attn, gain_ffn, gate_weight, up_weight, down_weight):
    block_index = (block_owner[:, 0] * CORP_DEV + slot_row).astype(jnp.int32)
    fetched = jnp.take(corpus, block_index, axis=0).reshape(NBLK * BLK, D)
    stream_in = jnp.concatenate([queries, fetched], axis=0)
    pair_ids = jnp.concatenate([jnp.arange(QROWS, dtype=jnp.int32) // QLEN, jnp.repeat(segment, BLK).astype(jnp.int32)])
    same_pair = pair_ids[:, None] == pair_ids[None, :]
    normal_in = normed(stream_in, gain_attn)

    def heads_of(weight):
        projected = by_rows(normal_in, weight).astype(jnp.bfloat16)
        return projected.reshape(TOK, HEADS, HDIM).transpose(1, 0, 2)
    stacked = (heads_of(query_weight), heads_of(key_weight), heads_of(value_weight))

    def one_head(head_parts):
        scores = jnp.dot(head_parts[0], head_parts[1].T, preferred_element_type=jnp.float32) * HDIM ** (-0.5)
        scores = jnp.where(same_pair, scores, -1e+30)
        row_max = lax.optimization_barrier(jnp.max(scores, axis=-1, keepdims=True))
        weights = jnp.exp(scores - row_max)
        probability = (weights / lax.optimization_barrier(jnp.sum(weights, axis=-1, keepdims=True))).astype(jnp.bfloat16)
        return jnp.dot(probability, head_parts[2], preferred_element_type=jnp.float32).astype(jnp.bfloat16)
    context = lax.map(one_head, stacked).transpose(1, 0, 2).reshape(TOK, HEADS * HDIM)
    attended = jnp.dot(context, out_weight, preferred_element_type=jnp.float32)
    stream_mid = (stream_in.astype(jnp.float32) + attended).astype(jnp.bfloat16)
    normal_mid = normed(stream_mid, gain_ffn)
    gate_value = by_rows(normal_mid, gate_weight)
    up_value = by_rows(normal_mid, up_weight)
    hidden = (jax.nn.gelu(gate_value, approximate=True) * up_value).astype(jnp.bfloat16)
    ffn_result = jnp.dot(hidden, down_weight, preferred_element_type=jnp.float32)
    return (stream_mid.astype(jnp.float32) + ffn_result).astype(jnp.bfloat16)
```

```python
import functools

import jax
import jax.numpy as jnp
from jax import lax
from jax.experimental import pallas as pl
from jax.experimental.pallas import tpu as pltpu
from jax.sharding import PartitionSpec as P

HDIM = 64
QLEN = 32
BLK = 4
CAP = 3


def normed(stream, gain):
    values = stream.astype(jnp.float32)
    mean_square = jnp.mean(values * values, axis=-1, keepdims=True)
    return (values * lax.rsqrt(mean_square + 1e-06) * gain).astype(jnp.bfloat16)


def by_rows(left, weight):
    return lax.dot_general(
        left, weight, (((1,), (1,)), ((), ())), preferred_element_type=jnp.float32
    )


def plain_body(
    queries,
    corpus,
    block_owner,
    slot_row,
    segment,
    query_weight,
    key_weight,
    value_weight,
    out_weight,
    gain_attn,
    gain_ffn,
    gate_weight,
    up_weight,
    down_weight,
):
    devices = lax.axis_size("tensor")
    my_index = lax.axis_index("tensor")
    owners = block_owner[:, 0]
    blocks_total = owners.shape[0]
    features = queries.shape[1]
    positions = jnp.arange(blocks_total, dtype=jnp.int32)
    earlier = (owners[:, None] == owners[None, :]) & (positions[:, None] < positions[None, :])
    slot_rank = jnp.sum(earlier.astype(jnp.int32), axis=0)
    slot_ids = jnp.arange(CAP, dtype=jnp.int32)
    choose_slot = (owners[None, :] == my_index) & (slot_rank[None, :] == slot_ids[:, None])
    local_rows = jnp.sum(jnp.where(choose_slot, slot_row[None, :], 0), axis=1)
    present = jnp.any(choose_slot, axis=1)
    outgoing = jnp.take(corpus, local_rows, axis=0)
    outgoing = jnp.where(present[:, None, None], outgoing, jnp.zeros_like(outgoing)).reshape(
        CAP, -1
    )
    location = owners * CAP + slot_rank
    query_all, arrived = (
        lax.all_gather(queries, "tensor", axis=0, tiled=True),
        lax.all_gather(outgoing, "tensor", axis=0, tiled=True),
    )
    stream_in = jnp.concatenate(
        [query_all, jnp.take(arrived, location, axis=0).reshape(-1, features)], axis=0
    )
    normal_rows = normed(stream_in, gain_attn)
    projected = tuple(
        (
            by_rows(normal_rows, weight).astype(jnp.bfloat16)
            for weight in (query_weight, key_weight, value_weight)
        )
    )
    tokens = stream_in.shape[0]
    heads_here = query_weight.shape[0] // HDIM
    query_rows_total = query_all.shape[0]
    pair_ids = jnp.concatenate(
        [jnp.arange(query_rows_total, dtype=jnp.int32) // QLEN, jnp.repeat(segment, BLK)]
    )
    same_pair = pair_ids[:, None] == pair_ids[None, :]
    query_heads = projected[0].reshape(tokens, heads_here, HDIM)
    key_heads = projected[1].reshape(tokens, heads_here, HDIM)
    value_heads = projected[2].reshape(tokens, heads_here, HDIM)
    scores = jnp.einsum(
        "qhd,khd->hqk", query_heads, key_heads, preferred_element_type=jnp.float32
    ) * HDIM ** (-0.5)
    scores = jnp.where(same_pair[None, :, :], scores, -1e30)
    row_max = jnp.max(scores, axis=-1, keepdims=True)
    weights = jnp.exp(scores - row_max)
    probability = (weights / jnp.sum(weights, axis=-1, keepdims=True)).astype(jnp.bfloat16)
    context = (
        jnp.einsum("hqk,khd->qhd", probability, value_heads, preferred_element_type=jnp.float32)
        .astype(jnp.bfloat16)
        .reshape(tokens, heads_here * HDIM)
    )
    rows_here = tokens // devices
    first_mine = my_index * rows_here
    attended = lax.psum(jnp.dot(context, out_weight, preferred_element_type=jnp.float32), "tensor")
    stream_mid = (stream_in.astype(jnp.float32) + attended).astype(jnp.bfloat16)
    normal_mid = normed(stream_mid, gain_ffn)
    mid_mine = lax.dynamic_slice_in_dim(stream_mid, first_mine, rows_here, 0)
    gate_value = by_rows(normal_mid, gate_weight)
    up_value = by_rows(normal_mid, up_weight)
    hidden = (jax.nn.gelu(gate_value, approximate=True) * up_value).astype(jnp.bfloat16)
    ffn_result = lax.psum_scatter(
        jnp.dot(hidden, down_weight, preferred_element_type=jnp.float32),
        "tensor",
        scatter_dimension=0,
        tiled=True,
    )
    return (mid_mine.astype(jnp.float32) + ffn_result).astype(jnp.bfloat16)


Z, Y, C = 4, 2, 2
SPLIT = 4
PAD = 16
MESH = pl.DeviceIdType.MESH


def fits(mesh):
    return mesh.shape["tensor"] == Z * Y * C


def fused_kernel(
    payload, wq, wk, wv, wo, wg, wu, wd, src_ref, pair_rows, pair_cols, gain1, gain2,
    out_ref,
    arrived, stream, normal, wqkv_v, wo_v, wg_v, wu_v, wd_v, ctx, hid, mid, gathered,
    part1, rcore1, s1a, ry1, s2a, rz1, part2, rcore2, s1b, ry2, s2b, rz2,
    wsem, ag1_s, ag1_r, ag2_s, ag2_r, rs1_s, rs1_r, rs2_s, rs2_r,
):
    me = lax.axis_index("tensor")
    z, y, c = me // (Y * C), (me // C) % Y, me % C

    def flat(zi, yi, ci):
        return zi * (Y * C) + yi * C + ci

    def line(dz):
        return (z + dz) % Z

    ypart = flat(z, 1 - y, c)
    cpart = flat(z, y, 1 - c)

    own = pltpu.make_async_copy(payload, arrived.at[me], wsem.at[0])
    own.start()
    loads = [
        pltpu.make_async_copy(src, dst, wsem.at[1 + i])
        for i, (src, dst) in enumerate(
            [
                (wq, wqkv_v.at[pl.ds(0, HDIM)]),
                (wk, wqkv_v.at[pl.ds(HDIM, HDIM)]),
                (wv, wqkv_v.at[pl.ds(2 * HDIM, HDIM)]),
                (wo, wo_v),
                (wg, wg_v),
                (wu, wu_v),
                (wd, wd_v),
            ]
        )
    ]
    for load in loads:
        load.start()

    barrier = pltpu.get_barrier_semaphore()
    for peer in [flat(line(dz), y, c) for dz in range(1, Z)] + [ypart, cpart]:
        pl.semaphore_signal(barrier, inc=1, device_id={"tensor": peer}, device_id_type=MESH)
    pl.semaphore_wait(barrier, Z + 1)

    def remote(src, dst, ssem, rsem, peer):
        return pltpu.make_async_remote_copy(
            src_ref=src, dst_ref=dst, send_sem=ssem, recv_sem=rsem,
            device_id={"tensor": peer}, device_id_type=MESH,
        )

    def gather(buf, ss, rs):
        ysem, csem = Z - 1, 2 * Z - 1
        sent = []

        def go(idx, sem, peer):
            copy = remote(buf.at[idx], buf.at[idx], ss.at[sem], rs.at[sem], peer)
            copy.start()
            sent.append(copy)

        def take(idx, sem, peer):
            remote(buf.at[idx], buf.at[idx], ss.at[sem], rs.at[sem], peer).wait_recv()

        for dz in range(1, Z):
            go(me, dz - 1, flat(line(dz), y, c))
        go(me, ysem, ypart)
        go(me, csem, cpart)
        for dz in range(1, Z):
            idx = flat(line(Z - dz), y, c)
            take(idx, dz - 1, idx)
            go(idx, ysem + dz, ypart)
            go(idx, csem + dz, cpart)
        for dz in range(Z):
            idx = flat(line(Z - dz), 1 - y, c)
            take(idx, ysem + dz, ypart)
            go(idx, csem + Z + dz, cpart)
        for dz in range(Z):
            for dy in range(Y):
                idx = flat(line(Z - dz), (y + dy) % Y, 1 - c)
                take(idx, csem + dy * Z + dz, cpart)
        return sent

    def scatter_sum(left, weight, part, rcore, s1, ry, s2, rz, ss, rs):
        features = weight.shape[1]
        tile = features // 4

        def core_copy(dz):
            return remote(part.at[line(dz), 1 - c], rcore.at[line(dz)], ss.at[dz], rs.at[dz], cpart)

        def row_copy(dz):
            return remote(s1.at[line(dz)], ry.at[line(dz)], ss.at[Z + dz], rs.at[Z + dz], ypart)

        def line_copy(dz):
            return remote(
                s2.at[dz - 1], rz.at[dz - 1], ss.at[2 * Z + dz - 1], rs.at[2 * Z + dz - 1],
                flat(line(dz), y, c),
            )

        def one(step, carry):
            dz = (step + 1) % Z
            zi = line(dz)
            rows = left[zi]
            for t in range(4):
                cols = pl.ds(t * tile, tile)
                found = jnp.dot(rows, weight[:, cols], preferred_element_type=jnp.float32)
                for yi in range(Y):
                    for ci in range(C):
                        at = (yi * C + ci) * PAD
                        part[zi, ci, yi, :, cols] = found[at : at + PAD].astype(jnp.bfloat16)
            core_copy(dz).start()
            return carry

        lax.fori_loop(0, Z, one, 0)
        order = list(range(1, Z)) + [0]

        def f32(v):
            return v.astype(jnp.float32)

        for dz in order:
            zi = line(dz)
            core_copy(dz).wait_recv()
            s1[zi] = (f32(part[zi, c, 1 - y]) + f32(rcore[zi, 1 - y])).astype(jnp.bfloat16)
            row_copy(dz).start()
        total = None
        for dz in order:
            zi = line(dz)
            row_copy(dz).wait_recv()
            value = f32(part[zi, c, y]) + f32(rcore[zi, y]) + f32(ry[zi])
            if dz:
                s2[dz - 1] = value.astype(jnp.bfloat16)
                line_copy(dz).start()
            else:
                total = value
        for dz in range(1, Z):
            line_copy(dz).wait_recv()
            total = total + f32(rz[dz - 1])
        for dz in range(Z):
            core_copy(dz).wait_send()
            row_copy(dz).wait_send()
            if dz:
                line_copy(dz).wait_send()
        return total

    own.wait()
    sent = gather(arrived, ag1_s, ag1_r)
    slots, features = arrived.shape[0] * arrived.shape[1], stream.shape[1]
    tokens = stream.shape[0]
    width = features // SPLIT
    per = arrived.shape[1] // SPLIT
    place = lax.broadcasted_iota(jnp.int32, (tokens, slots), 1)
    for j in range(SPLIT):
        chosen = (place == src_ref[...] + j * per).astype(jnp.float32).astype(jnp.bfloat16)
        stream[:, pl.ds(j * width, width)] = jnp.dot(
            chosen, arrived[...].reshape(slots, width), preferred_element_type=jnp.float32
        ).astype(jnp.bfloat16)

    def norm_rows(i, carry):
        at = pl.ds(pl.multiple_of(i * PAD, PAD), PAD)
        normal[at, :] = normed(stream[at, :], gain1[...])
        return carry

    lax.fori_loop(0, tokens // PAD, norm_rows, 0)
    for load in loads[:4]:
        load.wait()
    qkv = by_rows(normal[...], wqkv_v[...]).astype(jnp.bfloat16)
    q, k, v = qkv[:, :HDIM], qkv[:, HDIM : 2 * HDIM], qkv[:, 2 * HDIM :]
    scores = by_rows(q, k) * HDIM ** (-0.5)
    scores = jnp.where(pair_rows[...] == pair_cols[...], scores, -1e30)
    weights = jnp.exp(scores - jnp.max(scores, axis=-1, keepdims=True))
    probability = (weights / jnp.sum(weights, axis=-1, keepdims=True)).astype(jnp.bfloat16)
    context = jnp.dot(probability, v, preferred_element_type=jnp.float32).astype(jnp.bfloat16)
    ctx[...] = context.reshape(ctx.shape)
    for copy in sent:
        copy.wait_send()

    total = scatter_sum(ctx, wo_v, part1, rcore1, s1a, ry1, s2a, rz1, rs1_s, rs1_r)
    mine = stream[pl.ds(pl.multiple_of(me * PAD, PAD), PAD), :]
    mid[...] = (mine.astype(jnp.float32) + total).astype(jnp.bfloat16)
    gathered[me] = normed(mid[...], gain2[...])
    sent = gather(gathered, ag2_s, ag2_r)
    for load in loads[4:]:
        load.wait()
    rows = gathered[...].reshape(tokens, features)
    gate_value = by_rows(rows, wg_v[...])
    up_value = by_rows(rows, wu_v[...])
    hidden = (jax.nn.gelu(gate_value, approximate=True) * up_value).astype(jnp.bfloat16)
    hid[...] = hidden.reshape(hid.shape)
    for copy in sent:
        copy.wait_send()
    total = scatter_sum(hid, wd_v, part2, rcore2, s1b, ry2, s2b, rz2, rs2_s, rs2_r)
    out_ref[...] = (mid[...].astype(jnp.float32) + total)[: out_ref.shape[0]].astype(jnp.bfloat16)


def fused_body(
    queries, corpus, block_owner, slot_row, segment, query_weight, key_weight, value_weight,
    out_weight, gain_attn, gain_ffn, gate_weight, up_weight, down_weight,
):
    n = lax.axis_size("tensor")
    my_index = lax.axis_index("tensor")
    owners = block_owner[:, 0]
    blocks = owners.shape[0]
    query_rows, features = queries.shape
    per = query_rows + CAP * BLK
    tokens = n * query_rows + blocks * BLK
    rows_here = tokens // n
    positions = jnp.arange(blocks, dtype=jnp.int32)
    earlier = (owners[:, None] == owners[None, :]) & (positions[:, None] < positions[None, :])
    slot_rank = jnp.sum(earlier.astype(jnp.int32), axis=0)
    slot_ids = jnp.arange(CAP, dtype=jnp.int32)
    choose_slot = (owners[None, :] == my_index) & (slot_rank[None, :] == slot_ids[:, None])
    local_rows = jnp.sum(jnp.where(choose_slot, slot_row[None, :], 0), axis=1)
    outgoing = jnp.take(corpus, local_rows, axis=0).reshape(CAP * BLK, features)
    width = features // SPLIT
    payload = (
        jnp.concatenate([queries, outgoing], axis=0)
        .reshape(per, SPLIT, width)
        .transpose(1, 0, 2)
        .reshape(SPLIT * per, width)
    )
    query_ids = jnp.arange(n * query_rows, dtype=jnp.int32)
    starts = owners * (SPLIT * per) + query_rows + slot_rank * BLK
    token_ids = jnp.arange(BLK, dtype=jnp.int32)
    source = jnp.concatenate(
        [
            query_ids // query_rows * (SPLIT * per) + query_ids % query_rows,
            (starts[:, None] + token_ids[None, :]).reshape(-1),
        ]
    )
    pair = jnp.concatenate([query_ids // QLEN, jnp.repeat(segment, BLK)])

    def padded(v, fill):
        return jnp.pad(
            v.reshape(n, rows_here), ((0, 0), (0, PAD - rows_here)), constant_values=fill
        ).reshape(-1)

    source = padded(source, -(2**20))
    pair = padded(pair, -1)
    rows = n * PAD
    hidden = gate_weight.shape[0]
    bf = jnp.bfloat16
    chunk = (PAD, features)
    scatter_bufs = [
        pltpu.VMEM((Z, C, Y) + chunk, bf),
        pltpu.VMEM((Z, Y) + chunk, bf),
        pltpu.VMEM((Z,) + chunk, bf),
        pltpu.VMEM((Z,) + chunk, bf),
        pltpu.VMEM((Z - 1,) + chunk, bf),
        pltpu.VMEM((Z - 1,) + chunk, bf),
    ]
    dma = pltpu.SemaphoreType.DMA
    gather_sems = (2 * Z - 1 + Z * Y,)
    scatter_sems = (3 * Z - 1,)
    any_spec = pl.BlockSpec(memory_space=pl.ANY)
    vmem_spec = pl.BlockSpec(memory_space=pltpu.VMEM)
    return pl.pallas_call(
        fused_kernel,
        out_shape=jax.ShapeDtypeStruct((rows_here, features), bf),
        in_specs=[any_spec] * 8 + [vmem_spec] * 5,
        out_specs=vmem_spec,
        scratch_shapes=[
            pltpu.VMEM((n, SPLIT * per, width), bf),
            pltpu.VMEM((rows, features), bf),
            pltpu.VMEM((rows, features), bf),
            pltpu.VMEM((3 * HDIM, features), bf),
            pltpu.VMEM((HDIM, features), bf),
            pltpu.VMEM((hidden, features), bf),
            pltpu.VMEM((hidden, features), bf),
            pltpu.VMEM((hidden, features), bf),
            pltpu.VMEM((Z, rows // Z, HDIM), bf),
            pltpu.VMEM((Z, rows // Z, hidden), bf),
            pltpu.VMEM(chunk, bf),
            pltpu.VMEM((n,) + chunk, bf),
        ]
        + scatter_bufs
        + scatter_bufs
        + [dma((8,))]
        + [dma(gather_sems)] * 4
        + [dma(scatter_sems)] * 4,
        compiler_params=pltpu.CompilerParams(
            collective_id=0, has_side_effects=True, vmem_limit_bytes=56 * 2**20
        ),
    )(
        payload, query_weight, key_weight, value_weight, out_weight, gate_weight, up_weight,
        down_weight, source[:, None], pair[:, None], pair[None, :],
        gain_attn[None, :], gain_ffn[None, :],
    )


def solution(mesh):
    placed = (
        P(("groups", "tensor"), None),
        P(("groups", "tensor"), None, None),
        P("groups", None),
        P("groups"),
        P("groups"),
        P("tensor", None),
        P("tensor", None),
        P("tensor", None),
        P("tensor", None),
        P(),
        P(),
        P("tensor", None),
        P("tensor", None),
        P("tensor", None),
    )
    body = fused_body if fits(mesh) else plain_body
    return jax.shard_map(
        body, mesh=mesh, in_specs=placed, out_specs=P(("groups", "tensor"), None), check_vma=False
    )
```

```python
import functools

import jax
import jax.numpy as jnp
from jax import lax
from jax.experimental import pallas as pl
from jax.experimental.pallas import tpu as pltpu
from jax.sharding import PartitionSpec as P

HDIM = 64
QLEN = 32
BLK = 4
CAP = 3


def normed(stream, gain):
    values = stream.astype(jnp.float32)
    mean_square = jnp.mean(values * values, axis=-1, keepdims=True)
    return (values * lax.rsqrt(mean_square + 1e-06) * gain).astype(jnp.bfloat16)


def by_rows(left, weight):
    return lax.dot_general(
        left, weight, (((1,), (1,)), ((), ())), preferred_element_type=jnp.float32
    )


def plain_body(
    queries,
    corpus,
    block_owner,
    slot_row,
    segment,
    query_weight,
    key_weight,
    value_weight,
    out_weight,
    gain_attn,
    gain_ffn,
    gate_weight,
    up_weight,
    down_weight,
):
    devices = lax.axis_size("tensor")
    my_index = lax.axis_index("tensor")
    owners = block_owner[:, 0]
    blocks_total = owners.shape[0]
    features = queries.shape[1]
    positions = jnp.arange(blocks_total, dtype=jnp.int32)
    earlier = (owners[:, None] == owners[None, :]) & (positions[:, None] < positions[None, :])
    slot_rank = jnp.sum(earlier.astype(jnp.int32), axis=0)
    slot_ids = jnp.arange(CAP, dtype=jnp.int32)
    choose_slot = (owners[None, :] == my_index) & (slot_rank[None, :] == slot_ids[:, None])
    local_rows = jnp.sum(jnp.where(choose_slot, slot_row[None, :], 0), axis=1)
    present = jnp.any(choose_slot, axis=1)
    outgoing = jnp.take(corpus, local_rows, axis=0)
    outgoing = jnp.where(present[:, None, None], outgoing, jnp.zeros_like(outgoing)).reshape(
        CAP, -1
    )
    location = owners * CAP + slot_rank
    query_all, arrived = (
        lax.all_gather(queries, "tensor", axis=0, tiled=True),
        lax.all_gather(outgoing, "tensor", axis=0, tiled=True),
    )
    stream_in = jnp.concatenate(
        [query_all, jnp.take(arrived, location, axis=0).reshape(-1, features)], axis=0
    )
    normal_rows = normed(stream_in, gain_attn)
    projected = tuple(
        (
            by_rows(normal_rows, weight).astype(jnp.bfloat16)
            for weight in (query_weight, key_weight, value_weight)
        )
    )
    tokens = stream_in.shape[0]
    heads_here = query_weight.shape[0] // HDIM
    query_rows_total = query_all.shape[0]
    pair_ids = jnp.concatenate(
        [jnp.arange(query_rows_total, dtype=jnp.int32) // QLEN, jnp.repeat(segment, BLK)]
    )
    same_pair = pair_ids[:, None] == pair_ids[None, :]
    query_heads = projected[0].reshape(tokens, heads_here, HDIM)
    key_heads = projected[1].reshape(tokens, heads_here, HDIM)
    value_heads = projected[2].reshape(tokens, heads_here, HDIM)
    scores = jnp.einsum(
        "qhd,khd->hqk", query_heads, key_heads, preferred_element_type=jnp.float32
    ) * HDIM ** (-0.5)
    scores = jnp.where(same_pair[None, :, :], scores, -1e30)
    row_max = jnp.max(scores, axis=-1, keepdims=True)
    weights = jnp.exp(scores - row_max)
    probability = (weights / jnp.sum(weights, axis=-1, keepdims=True)).astype(jnp.bfloat16)
    context = (
        jnp.einsum("hqk,khd->qhd", probability, value_heads, preferred_element_type=jnp.float32)
        .astype(jnp.bfloat16)
        .reshape(tokens, heads_here * HDIM)
    )
    rows_here = tokens // devices
    first_mine = my_index * rows_here
    attended = lax.psum(jnp.dot(context, out_weight, preferred_element_type=jnp.float32), "tensor")
    stream_mid = (stream_in.astype(jnp.float32) + attended).astype(jnp.bfloat16)
    normal_mid = normed(stream_mid, gain_ffn)
    mid_mine = lax.dynamic_slice_in_dim(stream_mid, first_mine, rows_here, 0)
    gate_value = by_rows(normal_mid, gate_weight)
    up_value = by_rows(normal_mid, up_weight)
    hidden = (jax.nn.gelu(gate_value, approximate=True) * up_value).astype(jnp.bfloat16)
    ffn_result = lax.psum_scatter(
        jnp.dot(hidden, down_weight, preferred_element_type=jnp.float32),
        "tensor",
        scatter_dimension=0,
        tiled=True,
    )
    return (mid_mine.astype(jnp.float32) + ffn_result).astype(jnp.bfloat16)


Z, Y, C = 4, 2, 2
SPLIT = 4
PAD = 16
MESH = pl.DeviceIdType.MESH


def fits(mesh):
    return mesh.shape["tensor"] == Z * Y * C


def fused_kernel(
    payload, wq, wk, wv, wo, wg, wu, wd, src_ref, pair_rows, pair_cols, gain1, gain2,
    out_ref,
    arrived, stream, normal, wqkv_v, wo_v, wg_v, wu_v, wd_v, ctx, hid, mid, gathered,
    part1, rcore1, s1a, ry1, s2a, rz1, part2, rcore2, s1b, ry2, s2b, rz2,
    acc, summed, wsem, ag1_s, ag1_r, ag2_s, ag2_r, rs1_s, rs1_r, rs2_s, rs2_r,
):
    me = lax.axis_index("tensor")
    z, y, c = me // (Y * C), (me // C) % Y, me % C

    def flat(zi, yi, ci):
        return zi * (Y * C) + yi * C + ci

    ypart = flat(z, 1 - y, c)
    cpart = flat(z, y, 1 - c)

    own = pltpu.make_async_copy(payload, arrived.at[me], wsem.at[0])
    own.start()
    loads = [
        pltpu.make_async_copy(src, dst, wsem.at[1 + i])
        for i, (src, dst) in enumerate(
            [
                (wq, wqkv_v.at[pl.ds(0, HDIM)]),
                (wk, wqkv_v.at[pl.ds(HDIM, HDIM)]),
                (wv, wqkv_v.at[pl.ds(2 * HDIM, HDIM)]),
                (wo, wo_v),
                (wg, wg_v),
                (wu, wu_v),
                (wd, wd_v),
            ]
        )
    ]
    for load in loads:
        load.start()

    barrier = pltpu.get_barrier_semaphore()
    def greet(peer):
        pl.semaphore_signal(barrier, inc=1, device_id={"tensor": peer}, device_id_type=MESH)

    greet(ypart)
    greet(cpart)
    pl.when(z > 0)(lambda: greet(flat(z - 1, y, c)))
    pl.when(z + 1 < Z)(lambda: greet(flat(z + 1, y, c)))
    pl.semaphore_wait(barrier, jnp.where((z == 0) | (z + 1 == Z), 3, 4))

    def remote(src, dst, ssem, rsem, peer):
        return pltpu.make_async_remote_copy(
            src_ref=src, dst_ref=dst, send_sem=ssem, recv_sem=rsem,
            device_id={"tensor": peer}, device_id_type=MESH,
        )

    def gather(buf, ss, rs):
        lsem, ysem, csem = Z - 1, 2 * Z - 2, 3 * Z - 2

        def move(idx, sem, peer):
            return remote(buf.at[idx], buf.at[idx], ss.at[sem], rs.at[sem], peer)

        def right(s):
            return move(flat(z - s, y, c), s, flat(z + 1, y, c))

        def left(s):
            return move(flat(z + s, y, c), lsem + s, flat(z - 1, y, c))

        def row(zi):
            return move(flat(zi, y, c), ysem + zi, ypart)

        def core(zi, yi):
            return move(flat(zi, yi, c), csem + zi * Y + yi, cpart)

        def fan(zi):
            row(zi).start()
            core(zi, y).start()

        def from_row(zi):
            move(flat(zi, 1 - y, c), ysem + zi, ypart).wait_recv()
            core(zi, 1 - y).start()

        pl.when(z + 1 < Z)(lambda: right(0).start())
        pl.when(z > 0)(lambda: left(0).start())
        fan(z)
        for s in range(Z - 1):

            @pl.when(z - 1 - s >= 0)
            def _():
                zi = z - 1 - s
                move(flat(zi, y, c), s, flat(z - 1, y, c)).wait_recv()
                if s + 1 < Z - 1:
                    pl.when(z + 1 < Z)(lambda: right(s + 1).start())
                fan(zi)

            @pl.when(z + 1 + s < Z)
            def _():
                zi = z + 1 + s
                move(flat(zi, y, c), lsem + s, flat(z + 1, y, c)).wait_recv()
                if s + 1 < Z - 1:
                    pl.when(z > 0)(lambda: left(s + 1).start())
                fan(zi)

            pl.when(z - s >= 0)(lambda: from_row(z - s))
            if s:
                pl.when(z + s < Z)(lambda: from_row(z + s))
        pl.when(z - (Z - 1) >= 0)(lambda: from_row(z - (Z - 1)))
        pl.when(z + (Z - 1) < Z)(lambda: from_row(z + (Z - 1)))
        for zi in range(Z):
            for yi in range(Y):
                move(flat(zi, yi, 1 - c), csem + zi * Y + yi, cpart).wait_recv()

        def drain():
            for s in range(Z - 1):
                pl.when((z - s >= 0) & (z + 1 < Z))(lambda: right(s).wait_send())
                pl.when((z + s < Z) & (z > 0))(lambda: left(s).wait_send())
            for zi in range(Z):
                row(zi).wait_send()
                for yi in range(Y):
                    core(zi, yi).wait_send()

        return drain

    def scatter_sum(left, weight, part, rcore, s1, ry, s2, rz, ss, rs):
        features = weight.shape[1]
        tile = features // 4

        def place(i):
            return jnp.where(z < Z // 2, Z - 1 - i, i)

        def core_copy(zi):
            return remote(part.at[zi, 1 - c], rcore.at[zi], ss.at[zi], rs.at[zi], cpart)

        def row_copy(zi):
            return remote(s1.at[zi], ry.at[zi], ss.at[Z + zi], rs.at[Z + zi], ypart)

        def right_copy(zi, peer):
            sem = 2 * Z + zi
            return remote(s2.at[zi], rz.at[zi], ss.at[sem], rs.at[sem], flat(peer, y, c))

        def left_copy(zi, peer):
            sem = 3 * Z + zi
            return remote(s2.at[zi], rz.at[Z + zi], ss.at[sem], rs.at[sem], flat(peer, y, c))

        def f32(v):
            return v.astype(jnp.float32)

        def one(i, carry):
            zi = place(i)
            rows = left[zi]
            for t in range(4):
                cols = pl.ds(t * tile, tile)
                found = jnp.dot(rows, weight[:, cols], preferred_element_type=jnp.float32)
                for yi in range(Y):
                    for ci in range(C):
                        at = (yi * C + ci) * PAD
                        part[zi, ci, yi, :, cols] = found[at : at + PAD].astype(jnp.bfloat16)
            core_copy(zi).start()
            return carry

        lax.fori_loop(0, Z, one, 0)

        def two(i, carry):
            zi = place(i)
            core_copy(zi).wait_recv()
            s1[zi] = (f32(part[zi, c, 1 - y]) + f32(rcore[zi, 1 - y])).astype(jnp.bfloat16)
            row_copy(zi).start()
            return carry

        lax.fori_loop(0, Z, two, 0)

        def three(i, carry):
            zi = place(i)
            row_copy(zi).wait_recv()
            acc[...] = f32(part[zi, c, y]) + f32(rcore[zi, y]) + f32(ry[zi])

            @pl.when((zi > z) & (z > 0))
            def _():
                right_copy(zi, z - 1).wait_recv()
                acc[...] += f32(rz[zi])

            @pl.when((zi < z) & (z + 1 < Z))
            def _():
                left_copy(zi, z + 1).wait_recv()
                acc[...] += f32(rz[Z + zi])

            @pl.when(zi > z)
            def _():
                s2[zi] = acc[...].astype(jnp.bfloat16)
                right_copy(zi, z + 1).start()

            @pl.when(zi < z)
            def _():
                s2[zi] = acc[...].astype(jnp.bfloat16)
                left_copy(zi, z - 1).start()

            @pl.when(zi == z)
            def _():
                summed[...] = acc[...]

            return carry

        lax.fori_loop(0, Z, three, 0)

        @pl.when(z > 0)
        def _():
            right_copy(z, z - 1).wait_recv()
            summed[...] += f32(rz[z])

        @pl.when(z + 1 < Z)
        def _():
            left_copy(z, z + 1).wait_recv()
            summed[...] += f32(rz[Z + z])

        for zi in range(Z):
            core_copy(zi).wait_send()
            row_copy(zi).wait_send()
            pl.when(zi > z)(lambda: right_copy(zi, z + 1).wait_send())
            pl.when(zi < z)(lambda: left_copy(zi, z - 1).wait_send())
        return summed[...]

    own.wait()
    drain = gather(arrived, ag1_s, ag1_r)
    slots, features = arrived.shape[0] * arrived.shape[1], stream.shape[1]
    tokens = stream.shape[0]
    width = features // SPLIT
    per = arrived.shape[1] // SPLIT
    spot = lax.broadcasted_iota(jnp.int32, (tokens, slots), 1)
    for j in range(SPLIT):
        chosen = (spot == src_ref[...] + j * per).astype(jnp.float32).astype(jnp.bfloat16)
        stream[:, pl.ds(j * width, width)] = jnp.dot(
            chosen, arrived[...].reshape(slots, width), preferred_element_type=jnp.float32
        ).astype(jnp.bfloat16)

    def norm_rows(i, carry):
        at = pl.ds(pl.multiple_of(i * PAD, PAD), PAD)
        normal[at, :] = normed(stream[at, :], gain1[...])
        return carry

    lax.fori_loop(0, tokens // PAD, norm_rows, 0)
    for load in loads[:4]:
        load.wait()
    qkv = by_rows(normal[...], wqkv_v[...]).astype(jnp.bfloat16)
    q, k, v = qkv[:, :HDIM], qkv[:, HDIM : 2 * HDIM], qkv[:, 2 * HDIM :]
    scores = by_rows(q, k) * HDIM ** (-0.5)
    scores = jnp.where(pair_rows[...] == pair_cols[...], scores, -1e30)
    weights = jnp.exp(scores - jnp.max(scores, axis=-1, keepdims=True))
    probability = (weights / jnp.sum(weights, axis=-1, keepdims=True)).astype(jnp.bfloat16)
    context = jnp.dot(probability, v, preferred_element_type=jnp.float32).astype(jnp.bfloat16)
    ctx[...] = context.reshape(ctx.shape)
    drain()

    total = scatter_sum(ctx, wo_v, part1, rcore1, s1a, ry1, s2a, rz1, rs1_s, rs1_r)
    mine = stream[pl.ds(pl.multiple_of(me * PAD, PAD), PAD), :]
    mid[...] = (mine.astype(jnp.float32) + total).astype(jnp.bfloat16)
    gathered[me] = normed(mid[...], gain2[...])
    drain = gather(gathered, ag2_s, ag2_r)
    for load in loads[4:]:
        load.wait()
    rows = gathered[...].reshape(tokens, features)
    gate_value = by_rows(rows, wg_v[...])
    up_value = by_rows(rows, wu_v[...])
    hidden = (jax.nn.gelu(gate_value, approximate=True) * up_value).astype(jnp.bfloat16)
    hid[...] = hidden.reshape(hid.shape)
    drain()
    total = scatter_sum(hid, wd_v, part2, rcore2, s1b, ry2, s2b, rz2, rs2_s, rs2_r)
    out_ref[...] = (mid[...].astype(jnp.float32) + total)[: out_ref.shape[0]].astype(jnp.bfloat16)


def fused_body(
    queries, corpus, block_owner, slot_row, segment, query_weight, key_weight, value_weight,
    out_weight, gain_attn, gain_ffn, gate_weight, up_weight, down_weight,
):
    n = lax.axis_size("tensor")
    my_index = lax.axis_index("tensor")
    owners = block_owner[:, 0]
    blocks = owners.shape[0]
    query_rows, features = queries.shape
    per = query_rows + CAP * BLK
    tokens = n * query_rows + blocks * BLK
    rows_here = tokens // n
    positions = jnp.arange(blocks, dtype=jnp.int32)
    earlier = (owners[:, None] == owners[None, :]) & (positions[:, None] < positions[None, :])
    slot_rank = jnp.sum(earlier.astype(jnp.int32), axis=0)
    slot_ids = jnp.arange(CAP, dtype=jnp.int32)
    choose_slot = (owners[None, :] == my_index) & (slot_rank[None, :] == slot_ids[:, None])
    local_rows = jnp.sum(jnp.where(choose_slot, slot_row[None, :], 0), axis=1)
    outgoing = jnp.take(corpus, local_rows, axis=0).reshape(CAP * BLK, features)
    width = features // SPLIT
    payload = (
        jnp.concatenate([queries, outgoing], axis=0)
        .reshape(per, SPLIT, width)
        .transpose(1, 0, 2)
        .reshape(SPLIT * per, width)
    )
    query_ids = jnp.arange(n * query_rows, dtype=jnp.int32)
    starts = owners * (SPLIT * per) + query_rows + slot_rank * BLK
    token_ids = jnp.arange(BLK, dtype=jnp.int32)
    source = jnp.concatenate(
        [
            query_ids // query_rows * (SPLIT * per) + query_ids % query_rows,
            (starts[:, None] + token_ids[None, :]).reshape(-1),
        ]
    )
    pair = jnp.concatenate([query_ids // QLEN, jnp.repeat(segment, BLK)])

    def padded(v, fill):
        return jnp.pad(
            v.reshape(n, rows_here), ((0, 0), (0, PAD - rows_here)), constant_values=fill
        ).reshape(-1)

    source = padded(source, -(2**20))
    pair = padded(pair, -1)
    rows = n * PAD
    hidden = gate_weight.shape[0]
    bf = jnp.bfloat16
    chunk = (PAD, features)
    scatter_bufs = [
        pltpu.VMEM((Z, C, Y) + chunk, bf),
        pltpu.VMEM((Z, Y) + chunk, bf),
        pltpu.VMEM((Z,) + chunk, bf),
        pltpu.VMEM((Z,) + chunk, bf),
        pltpu.VMEM((Z,) + chunk, bf),
        pltpu.VMEM((2 * Z,) + chunk, bf),
    ]
    dma = pltpu.SemaphoreType.DMA
    gather_sems = (3 * Z - 2 + Z * Y,)
    scatter_sems = (4 * Z,)
    any_spec = pl.BlockSpec(memory_space=pl.ANY)
    vmem_spec = pl.BlockSpec(memory_space=pltpu.VMEM)
    return pl.pallas_call(
        fused_kernel,
        out_shape=jax.ShapeDtypeStruct((rows_here, features), bf),
        in_specs=[any_spec] * 8 + [vmem_spec] * 5,
        out_specs=vmem_spec,
        scratch_shapes=[
            pltpu.VMEM((n, SPLIT * per, width), bf),
            pltpu.VMEM((rows, features), bf),
            pltpu.VMEM((rows, features), bf),
            pltpu.VMEM((3 * HDIM, features), bf),
            pltpu.VMEM((HDIM, features), bf),
            pltpu.VMEM((hidden, features), bf),
            pltpu.VMEM((hidden, features), bf),
            pltpu.VMEM((hidden, features), bf),
            pltpu.VMEM((Z, rows // Z, HDIM), bf),
            pltpu.VMEM((Z, rows // Z, hidden), bf),
            pltpu.VMEM(chunk, bf),
            pltpu.VMEM((n,) + chunk, bf),
        ]
        + scatter_bufs
        + scatter_bufs
        + [pltpu.VMEM(chunk, jnp.float32)] * 2
        + [dma((8,))]
        + [dma(gather_sems)] * 4
        + [dma(scatter_sems)] * 4,
        compiler_params=pltpu.CompilerParams(
            collective_id=0, has_side_effects=True, vmem_limit_bytes=56 * 2**20
        ),
    )(
        payload, query_weight, key_weight, value_weight, out_weight, gate_weight, up_weight,
        down_weight, source[:, None], pair[:, None], pair[None, :],
        gain_attn[None, :], gain_ffn[None, :],
    )


def solution(mesh):
    placed = (
        P(("groups", "tensor"), None),
        P(("groups", "tensor"), None, None),
        P("groups", None),
        P("groups"),
        P("groups"),
        P("tensor", None),
        P("tensor", None),
        P("tensor", None),
        P("tensor", None),
        P(),
        P(),
        P("tensor", None),
        P("tensor", None),
        P("tensor", None),
    )
    body = fused_body if fits(mesh) else plain_body
    return jax.shard_map(
        body, mesh=mesh, in_specs=placed, out_specs=P(("groups", "tensor"), None), check_vma=False
    )
```

```python
import functools

import jax
import jax.numpy as jnp
from jax import lax
from jax.experimental import pallas as pl
from jax.experimental.pallas import tpu as pltpu
from jax.sharding import PartitionSpec as P

HDIM = 64
QLEN = 32
BLK = 4
CAP = 3


def normed(stream, gain):
    values = stream.astype(jnp.float32)
    mean_square = jnp.mean(values * values, axis=-1, keepdims=True)
    return (values * lax.rsqrt(mean_square + 1e-06) * gain).astype(jnp.bfloat16)


def by_rows(left, weight):
    return lax.dot_general(
        left, weight, (((1,), (1,)), ((), ())), preferred_element_type=jnp.float32
    )


def plain_body(
    queries,
    corpus,
    block_owner,
    slot_row,
    segment,
    query_weight,
    key_weight,
    value_weight,
    out_weight,
    gain_attn,
    gain_ffn,
    gate_weight,
    up_weight,
    down_weight,
):
    devices = lax.axis_size("tensor")
    my_index = lax.axis_index("tensor")
    owners = block_owner[:, 0]
    blocks_total = owners.shape[0]
    features = queries.shape[1]
    positions = jnp.arange(blocks_total, dtype=jnp.int32)
    earlier = (owners[:, None] == owners[None, :]) & (positions[:, None] < positions[None, :])
    slot_rank = jnp.sum(earlier.astype(jnp.int32), axis=0)
    slot_ids = jnp.arange(CAP, dtype=jnp.int32)
    choose_slot = (owners[None, :] == my_index) & (slot_rank[None, :] == slot_ids[:, None])
    local_rows = jnp.sum(jnp.where(choose_slot, slot_row[None, :], 0), axis=1)
    present = jnp.any(choose_slot, axis=1)
    outgoing = jnp.take(corpus, local_rows, axis=0)
    outgoing = jnp.where(present[:, None, None], outgoing, jnp.zeros_like(outgoing)).reshape(
        CAP, -1
    )
    location = owners * CAP + slot_rank
    query_all, arrived = (
        lax.all_gather(queries, "tensor", axis=0, tiled=True),
        lax.all_gather(outgoing, "tensor", axis=0, tiled=True),
    )
    stream_in = jnp.concatenate(
        [query_all, jnp.take(arrived, location, axis=0).reshape(-1, features)], axis=0
    )
    normal_rows = normed(stream_in, gain_attn)
    projected = tuple(
        (
            by_rows(normal_rows, weight).astype(jnp.bfloat16)
            for weight in (query_weight, key_weight, value_weight)
        )
    )
    tokens = stream_in.shape[0]
    heads_here = query_weight.shape[0] // HDIM
    query_rows_total = query_all.shape[0]
    pair_ids = jnp.concatenate(
        [jnp.arange(query_rows_total, dtype=jnp.int32) // QLEN, jnp.repeat(segment, BLK)]
    )
    same_pair = pair_ids[:, None] == pair_ids[None, :]
    query_heads = projected[0].reshape(tokens, heads_here, HDIM)
    key_heads = projected[1].reshape(tokens, heads_here, HDIM)
    value_heads = projected[2].reshape(tokens, heads_here, HDIM)
    scores = jnp.einsum(
        "qhd,khd->hqk", query_heads, key_heads, preferred_element_type=jnp.float32
    ) * HDIM ** (-0.5)
    scores = jnp.where(same_pair[None, :, :], scores, -1e30)
    row_max = jnp.max(scores, axis=-1, keepdims=True)
    weights = jnp.exp(scores - row_max)
    probability = (weights / jnp.sum(weights, axis=-1, keepdims=True)).astype(jnp.bfloat16)
    context = (
        jnp.einsum("hqk,khd->qhd", probability, value_heads, preferred_element_type=jnp.float32)
        .astype(jnp.bfloat16)
        .reshape(tokens, heads_here * HDIM)
    )
    rows_here = tokens // devices
    first_mine = my_index * rows_here
    attended = lax.psum(jnp.dot(context, out_weight, preferred_element_type=jnp.float32), "tensor")
    stream_mid = (stream_in.astype(jnp.float32) + attended).astype(jnp.bfloat16)
    normal_mid = normed(stream_mid, gain_ffn)
    mid_mine = lax.dynamic_slice_in_dim(stream_mid, first_mine, rows_here, 0)
    gate_value = by_rows(normal_mid, gate_weight)
    up_value = by_rows(normal_mid, up_weight)
    hidden = (jax.nn.gelu(gate_value, approximate=True) * up_value).astype(jnp.bfloat16)
    ffn_result = lax.psum_scatter(
        jnp.dot(hidden, down_weight, preferred_element_type=jnp.float32),
        "tensor",
        scatter_dimension=0,
        tiled=True,
    )
    return (mid_mine.astype(jnp.float32) + ffn_result).astype(jnp.bfloat16)


Z, Y, C = 4, 2, 2
SPLIT = 4
HALVES = 2
PAD = 8
MESH = pl.DeviceIdType.MESH


def fits(mesh):
    return mesh.shape["tensor"] == Z * Y * C


def fused_kernel(
    payload, wq, wk, wv, wo, wg, wu, wd, src_ref, pair_rows, pair_cols, gain1, gain2,
    out_ref,
    arrived, stream, normal, wqkv_v, wo_v, wg_v, wu_v, wd_v, ctx, hid, mid, gathered,
    part1, rcore1, s1a, ry1, s2a, rz1, part2, rcore2, s1b, ry2, s2b, rz2,
    acc, summed, wsem, ag1_s, ag1_r, ag2_s, ag2_r, rs1_s, rs1_r, rs2_s, rs2_r,
):
    me = lax.axis_index("tensor")
    z, y, c = me // (Y * C), (me // C) % Y, me % C

    def flat(zi, yi, ci):
        return zi * (Y * C) + yi * C + ci

    ypart = flat(z, 1 - y, c)
    cpart = flat(z, y, 1 - c)

    own = pltpu.make_async_copy(payload, arrived.at[me], wsem.at[0])
    own.start()
    loads = [
        pltpu.make_async_copy(src, dst, wsem.at[1 + i])
        for i, (src, dst) in enumerate(
            [
                (wq, wqkv_v.at[pl.ds(0, HDIM)]),
                (wk, wqkv_v.at[pl.ds(HDIM, HDIM)]),
                (wv, wqkv_v.at[pl.ds(2 * HDIM, HDIM)]),
                (wo, wo_v),
                (wg, wg_v),
                (wu, wu_v),
                (wd, wd_v),
            ]
        )
    ]
    for load in loads:
        load.start()

    barrier = pltpu.get_barrier_semaphore()
    def greet(peer):
        pl.semaphore_signal(barrier, inc=1, device_id={"tensor": peer}, device_id_type=MESH)

    greet(ypart)
    greet(cpart)
    pl.when(z > 0)(lambda: greet(flat(z - 1, y, c)))
    pl.when(z + 1 < Z)(lambda: greet(flat(z + 1, y, c)))
    pl.semaphore_wait(barrier, jnp.where((z == 0) | (z + 1 == Z), 3, 4))

    def remote(src, dst, ssem, rsem, peer):
        return pltpu.make_async_remote_copy(
            src_ref=src, dst_ref=dst, send_sem=ssem, recv_sem=rsem,
            device_id={"tensor": peer}, device_id_type=MESH,
        )

    def gather(at, ss, rs):
        lsem, ysem, csem = Z - 1, 2 * Z - 2, 3 * Z - 2

        def move(idx, sem, peer):
            return remote(at(idx), at(idx), ss.at[sem], rs.at[sem], peer)

        def right(s):
            return move(flat(z - s, y, c), s, flat(z + 1, y, c))

        def left(s):
            return move(flat(z + s, y, c), lsem + s, flat(z - 1, y, c))

        def row(zi):
            return move(flat(zi, y, c), ysem + zi, ypart)

        def core(zi, yi):
            return move(flat(zi, yi, c), csem + zi * Y + yi, cpart)

        def fan(zi):
            row(zi).start()
            core(zi, y).start()

        def from_row(zi):
            move(flat(zi, 1 - y, c), ysem + zi, ypart).wait_recv()
            core(zi, 1 - y).start()

        def begin():
            pl.when(z + 1 < Z)(lambda: right(0).start())
            pl.when(z > 0)(lambda: left(0).start())
            fan(z)

        def progress():
            for s in range(Z - 1):

                @pl.when(z - 1 - s >= 0)
                def _():
                    zi = z - 1 - s
                    move(flat(zi, y, c), s, flat(z - 1, y, c)).wait_recv()
                    if s + 1 < Z - 1:
                        pl.when(z + 1 < Z)(lambda: right(s + 1).start())
                    fan(zi)

                @pl.when(z + 1 + s < Z)
                def _():
                    zi = z + 1 + s
                    move(flat(zi, y, c), lsem + s, flat(z + 1, y, c)).wait_recv()
                    if s + 1 < Z - 1:
                        pl.when(z > 0)(lambda: left(s + 1).start())
                    fan(zi)

                pl.when(z - s >= 0)(lambda: from_row(z - s))
                if s:
                    pl.when(z + s < Z)(lambda: from_row(z + s))
            pl.when(z - (Z - 1) >= 0)(lambda: from_row(z - (Z - 1)))
            pl.when(z + (Z - 1) < Z)(lambda: from_row(z + (Z - 1)))
            for zi in range(Z):
                for yi in range(Y):
                    move(flat(zi, yi, 1 - c), csem + zi * Y + yi, cpart).wait_recv()

        def drain():
            for s in range(Z - 1):
                pl.when((z - s >= 0) & (z + 1 < Z))(lambda: right(s).wait_send())
                pl.when((z + s < Z) & (z > 0))(lambda: left(s).wait_send())
            for zi in range(Z):
                row(zi).wait_send()
                for yi in range(Y):
                    core(zi, yi).wait_send()

        return begin, progress, drain

    def scatter_sum(left, weight, part, rcore, s1, ry, s2, rz, ss, rs):
        features = weight.shape[1]
        tile = features // 4

        def place(i):
            return jnp.where(z < Z // 2, Z - 1 - i, i)

        def core_copy(zi):
            return remote(part.at[zi, 1 - c], rcore.at[zi], ss.at[zi], rs.at[zi], cpart)

        def row_copy(zi):
            return remote(s1.at[zi], ry.at[zi], ss.at[Z + zi], rs.at[Z + zi], ypart)

        def right_copy(zi, peer):
            sem = 2 * Z + zi
            return remote(s2.at[zi], rz.at[zi], ss.at[sem], rs.at[sem], flat(peer, y, c))

        def left_copy(zi, peer):
            sem = 3 * Z + zi
            return remote(s2.at[zi], rz.at[Z + zi], ss.at[sem], rs.at[sem], flat(peer, y, c))

        def f32(v):
            return v.astype(jnp.float32)

        def multiply():
            rows = left[...]
            for t in range(4):
                cols = pl.ds(t * tile, tile)
                found = jnp.dot(rows, weight[:, cols], preferred_element_type=jnp.float32)
                for zi in range(Z):
                    for yi in range(Y):
                        for ci in range(C):
                            at = flat(zi, yi, ci) * PAD
                            part[zi, ci, yi, :, cols] = found[at : at + PAD].astype(jnp.bfloat16)
            for i in range(Z):
                core_copy(place(i)).start()

        def two(i, carry):
            zi = place(i)
            core_copy(zi).wait_recv()
            s1[zi] = (f32(part[zi, c, 1 - y]) + f32(rcore[zi, 1 - y])).astype(jnp.bfloat16)
            row_copy(zi).start()
            return carry

        def three(i, carry):
            zi = place(i)
            row_copy(zi).wait_recv()
            acc[...] = f32(part[zi, c, y]) + f32(rcore[zi, y]) + f32(ry[zi])

            @pl.when((zi > z) & (z > 0))
            def _():
                right_copy(zi, z - 1).wait_recv()
                acc[...] += f32(rz[zi])

            @pl.when((zi < z) & (z + 1 < Z))
            def _():
                left_copy(zi, z + 1).wait_recv()
                acc[...] += f32(rz[Z + zi])

            @pl.when(zi > z)
            def _():
                s2[zi] = acc[...].astype(jnp.bfloat16)
                right_copy(zi, z + 1).start()

            @pl.when(zi < z)
            def _():
                s2[zi] = acc[...].astype(jnp.bfloat16)
                left_copy(zi, z - 1).start()

            @pl.when(zi == z)
            def _():
                summed[...] = acc[...]

            return carry

        def spread():
            lax.fori_loop(0, Z, two, 0)

        def finish():
            lax.fori_loop(0, Z, three, 0)

            @pl.when(z > 0)
            def _():
                right_copy(z, z - 1).wait_recv()
                summed[...] += f32(rz[z])

            @pl.when(z + 1 < Z)
            def _():
                left_copy(z, z + 1).wait_recv()
                summed[...] += f32(rz[Z + z])
            return summed[...]

        def drain():
            for zi in range(Z):
                core_copy(zi).wait_send()
                row_copy(zi).wait_send()
                pl.when(zi > z)(lambda: right_copy(zi, z + 1).wait_send())
                pl.when(zi < z)(lambda: left_copy(zi, z - 1).wait_send())

        return multiply, spread, finish, drain

    own.wait()
    begin, progress, drain_in = gather(lambda idx: arrived.at[idx], ag1_s, ag1_r)
    begin()
    progress()
    slots, features = arrived.shape[0] * arrived.shape[1], stream.shape[1]
    tokens = stream.shape[0]
    width = features // SPLIT
    per = arrived.shape[1] // SPLIT
    spot = lax.broadcasted_iota(jnp.int32, (tokens, slots), 1)
    for j in range(SPLIT):
        chosen = (spot == src_ref[...] + j * per).astype(jnp.float32).astype(jnp.bfloat16)
        stream[:, pl.ds(j * width, width)] = jnp.dot(
            chosen, arrived[...].reshape(slots, width), preferred_element_type=jnp.float32
        ).astype(jnp.bfloat16)

    def norm_rows(i, carry):
        at = pl.ds(pl.multiple_of(i * 16, 16), 16)
        normal[at, :] = normed(stream[at, :], gain1[...])
        return carry

    lax.fori_loop(0, tokens // 16, norm_rows, 0)
    for load in loads[:4]:
        load.wait()
    qkv = by_rows(normal[...], wqkv_v[...]).astype(jnp.bfloat16)
    q, k, v = qkv[:, :HDIM], qkv[:, HDIM : 2 * HDIM], qkv[:, 2 * HDIM :]
    scores = by_rows(q, k) * HDIM ** (-0.5)
    scores = jnp.where(pair_rows[...] == pair_cols[...], scores, -1e30)
    weights = jnp.exp(scores - jnp.max(scores, axis=-1, keepdims=True))
    probability = (weights / jnp.sum(weights, axis=-1, keepdims=True)).astype(jnp.bfloat16)
    context = jnp.dot(probability, v, preferred_element_type=jnp.float32).astype(jnp.bfloat16)
    ctx[...] = context.reshape(ctx.shape)
    half = tokens // HALVES

    def rows_of(h, idx):
        return gathered.at[h, pl.ds(pl.multiple_of(idx * PAD, PAD), PAD)]

    attend, share, forward, output = [], [], [], []
    for h in range(HALVES):
        attend.append(scatter_sum(
            ctx.at[h], wo_v, part1.at[h], rcore1.at[h], s1a.at[h], ry1.at[h], s2a.at[h],
            rz1.at[h], rs1_s.at[h], rs1_r.at[h],
        ))
        share.append(gather(functools.partial(rows_of, h), ag2_s.at[h], ag2_r.at[h]))
        output.append(scatter_sum(
            hid.at[h], wd_v, part2.at[h], rcore2.at[h], s1b.at[h], ry2.at[h], s2b.at[h],
            rz2.at[h], rs2_s.at[h], rs2_r.at[h],
        ))

    def feed(h):
        rows = gathered[h]
        gate_value = by_rows(rows, wg_v[...])
        up_value = by_rows(rows, wu_v[...])
        hid[h] = (jax.nn.gelu(gate_value, approximate=True) * up_value).astype(jnp.bfloat16)

    for h in range(HALVES):
        attend[h][0]()
    for h in range(HALVES):
        attend[h][1]()
    for h in range(HALVES):
        total = attend[h][2]()
        mine = stream[pl.ds(pl.multiple_of(h * half + me * PAD, PAD), PAD), :]
        mid[h] = (mine.astype(jnp.float32) + total).astype(jnp.bfloat16)
        gathered[h, pl.ds(pl.multiple_of(me * PAD, PAD), PAD), :] = normed(mid[h], gain2[...])
        share[h][0]()
    for load in loads[4:]:
        load.wait()
    for h in range(HALVES):
        share[h][1]()
        if h:
            output[h - 1][1]()
        feed(h)
        output[h][0]()
    output[HALVES - 1][1]()
    kept = out_ref.shape[0]
    for h in range(HALVES):
        total = output[h][2]()
        top = min(PAD, kept - h * PAD)
        value = mid[h].astype(jnp.float32) + total
        out_ref[pl.ds(h * PAD, top), :] = value[:top].astype(jnp.bfloat16)
    drain_in()
    for h in range(HALVES):
        attend[h][3]()
        share[h][2]()
        output[h][3]()


def fused_body(
    queries, corpus, block_owner, slot_row, segment, query_weight, key_weight, value_weight,
    out_weight, gain_attn, gain_ffn, gate_weight, up_weight, down_weight,
):
    n = lax.axis_size("tensor")
    my_index = lax.axis_index("tensor")
    owners = block_owner[:, 0]
    blocks = owners.shape[0]
    query_rows, features = queries.shape
    per = query_rows + CAP * BLK
    tokens = n * query_rows + blocks * BLK
    rows_here = tokens // n
    positions = jnp.arange(blocks, dtype=jnp.int32)
    earlier = (owners[:, None] == owners[None, :]) & (positions[:, None] < positions[None, :])
    slot_rank = jnp.sum(earlier.astype(jnp.int32), axis=0)
    slot_ids = jnp.arange(CAP, dtype=jnp.int32)
    choose_slot = (owners[None, :] == my_index) & (slot_rank[None, :] == slot_ids[:, None])
    local_rows = jnp.sum(jnp.where(choose_slot, slot_row[None, :], 0), axis=1)
    outgoing = jnp.take(corpus, local_rows, axis=0).reshape(CAP * BLK, features)
    width = features // SPLIT
    payload = (
        jnp.concatenate([queries, outgoing], axis=0)
        .reshape(per, SPLIT, width)
        .transpose(1, 0, 2)
        .reshape(SPLIT * per, width)
    )
    query_ids = jnp.arange(n * query_rows, dtype=jnp.int32)
    starts = owners * (SPLIT * per) + query_rows + slot_rank * BLK
    token_ids = jnp.arange(BLK, dtype=jnp.int32)
    source = jnp.concatenate(
        [
            query_ids // query_rows * (SPLIT * per) + query_ids % query_rows,
            (starts[:, None] + token_ids[None, :]).reshape(-1),
        ]
    )
    pair = jnp.concatenate([query_ids // QLEN, jnp.repeat(segment, BLK)])

    def padded(v, fill):
        filled = jnp.pad(
            v.reshape(n, rows_here),
            ((0, 0), (0, HALVES * PAD - rows_here)),
            constant_values=fill,
        )
        return filled.reshape(n, HALVES, PAD).transpose(1, 0, 2).reshape(-1)

    source = padded(source, -(2**20))
    pair = padded(pair, -1)
    rows = n * HALVES * PAD
    hidden = gate_weight.shape[0]
    bf = jnp.bfloat16
    chunk = (PAD, features)
    scatter_bufs = [
        pltpu.VMEM((HALVES, Z, C, Y) + chunk, bf),
        pltpu.VMEM((HALVES, Z, Y) + chunk, bf),
        pltpu.VMEM((HALVES, Z) + chunk, bf),
        pltpu.VMEM((HALVES, Z) + chunk, bf),
        pltpu.VMEM((HALVES, Z) + chunk, bf),
        pltpu.VMEM((HALVES, 2 * Z) + chunk, bf),
    ]
    dma = pltpu.SemaphoreType.DMA
    gather_sems = 3 * Z - 2 + Z * Y
    scatter_sems = 4 * Z
    any_spec = pl.BlockSpec(memory_space=pl.ANY)
    vmem_spec = pl.BlockSpec(memory_space=pltpu.VMEM)
    return pl.pallas_call(
        fused_kernel,
        out_shape=jax.ShapeDtypeStruct((rows_here, features), bf),
        in_specs=[any_spec] * 8 + [vmem_spec] * 5,
        out_specs=vmem_spec,
        scratch_shapes=[
            pltpu.VMEM((n, SPLIT * per, width), bf),
            pltpu.VMEM((rows, features), bf),
            pltpu.VMEM((rows, features), bf),
            pltpu.VMEM((3 * HDIM, features), bf),
            pltpu.VMEM((HDIM, features), bf),
            pltpu.VMEM((hidden, features), bf),
            pltpu.VMEM((hidden, features), bf),
            pltpu.VMEM((hidden, features), bf),
            pltpu.VMEM((HALVES, rows // HALVES, HDIM), bf),
            pltpu.VMEM((HALVES, rows // HALVES, hidden), bf),
            pltpu.VMEM((HALVES,) + chunk, bf),
            pltpu.VMEM((HALVES, rows // HALVES, features), bf),
        ]
        + scatter_bufs
        + scatter_bufs
        + [pltpu.VMEM(chunk, jnp.float32)] * 2
        + [dma((8,))]
        + [dma((gather_sems,))] * 2
        + [dma((HALVES, gather_sems))] * 2
        + [dma((HALVES, scatter_sems))] * 4,
        compiler_params=pltpu.CompilerParams(
            collective_id=0, has_side_effects=True, vmem_limit_bytes=56 * 2**20
        ),
    )(
        payload, query_weight, key_weight, value_weight, out_weight, gate_weight, up_weight,
        down_weight, source[:, None], pair[:, None], pair[None, :],
        gain_attn[None, :], gain_ffn[None, :],
    )


def solution(mesh):
    placed = (
        P(("groups", "tensor"), None),
        P(("groups", "tensor"), None, None),
        P("groups", None),
        P("groups"),
        P("groups"),
        P("tensor", None),
        P("tensor", None),
        P("tensor", None),
        P("tensor", None),
        P(),
        P(),
        P("tensor", None),
        P("tensor", None),
        P("tensor", None),
    )
    body = fused_body if fits(mesh) else plain_body
    return jax.shard_map(
        body, mesh=mesh, in_specs=placed, out_specs=P(("groups", "tensor"), None), check_vma=False
    )
```

```python
import functools

import jax
import jax.numpy as jnp
from jax import lax
from jax.experimental import pallas as pl
from jax.experimental.pallas import tpu as pltpu
from jax.sharding import PartitionSpec as P

HDIM = 64
QLEN = 32
BLK = 4
CAP = 3


def normed(stream, gain):
    values = stream.astype(jnp.float32)
    mean_square = jnp.mean(values * values, axis=-1, keepdims=True)
    return (values * lax.rsqrt(mean_square + 1e-06) * gain).astype(jnp.bfloat16)


def by_rows(left, weight):
    return lax.dot_general(
        left, weight, (((1,), (1,)), ((), ())), preferred_element_type=jnp.float32
    )


def plain_body(
    queries,
    corpus,
    block_owner,
    slot_row,
    segment,
    query_weight,
    key_weight,
    value_weight,
    out_weight,
    gain_attn,
    gain_ffn,
    gate_weight,
    up_weight,
    down_weight,
):
    devices = lax.axis_size("tensor")
    my_index = lax.axis_index("tensor")
    owners = block_owner[:, 0]
    blocks_total = owners.shape[0]
    features = queries.shape[1]
    positions = jnp.arange(blocks_total, dtype=jnp.int32)
    earlier = (owners[:, None] == owners[None, :]) & (positions[:, None] < positions[None, :])
    slot_rank = jnp.sum(earlier.astype(jnp.int32), axis=0)
    slot_ids = jnp.arange(CAP, dtype=jnp.int32)
    choose_slot = (owners[None, :] == my_index) & (slot_rank[None, :] == slot_ids[:, None])
    local_rows = jnp.sum(jnp.where(choose_slot, slot_row[None, :], 0), axis=1)
    present = jnp.any(choose_slot, axis=1)
    outgoing = jnp.take(corpus, local_rows, axis=0)
    outgoing = jnp.where(present[:, None, None], outgoing, jnp.zeros_like(outgoing)).reshape(
        CAP, -1
    )
    location = owners * CAP + slot_rank
    query_all, arrived = (
        lax.all_gather(queries, "tensor", axis=0, tiled=True),
        lax.all_gather(outgoing, "tensor", axis=0, tiled=True),
    )
    stream_in = jnp.concatenate(
        [query_all, jnp.take(arrived, location, axis=0).reshape(-1, features)], axis=0
    )
    normal_rows = normed(stream_in, gain_attn)
    projected = tuple(
        (
            by_rows(normal_rows, weight).astype(jnp.bfloat16)
            for weight in (query_weight, key_weight, value_weight)
        )
    )
    tokens = stream_in.shape[0]
    heads_here = query_weight.shape[0] // HDIM
    query_rows_total = query_all.shape[0]
    pair_ids = jnp.concatenate(
        [jnp.arange(query_rows_total, dtype=jnp.int32) // QLEN, jnp.repeat(segment, BLK)]
    )
    same_pair = pair_ids[:, None] == pair_ids[None, :]
    query_heads = projected[0].reshape(tokens, heads_here, HDIM)
    key_heads = projected[1].reshape(tokens, heads_here, HDIM)
    value_heads = projected[2].reshape(tokens, heads_here, HDIM)
    scores = jnp.einsum(
        "qhd,khd->hqk", query_heads, key_heads, preferred_element_type=jnp.float32
    ) * HDIM ** (-0.5)
    scores = jnp.where(same_pair[None, :, :], scores, -1e30)
    row_max = jnp.max(scores, axis=-1, keepdims=True)
    weights = jnp.exp(scores - row_max)
    probability = (weights / jnp.sum(weights, axis=-1, keepdims=True)).astype(jnp.bfloat16)
    context = (
        jnp.einsum("hqk,khd->qhd", probability, value_heads, preferred_element_type=jnp.float32)
        .astype(jnp.bfloat16)
        .reshape(tokens, heads_here * HDIM)
    )
    rows_here = tokens // devices
    first_mine = my_index * rows_here
    attended = lax.psum(jnp.dot(context, out_weight, preferred_element_type=jnp.float32), "tensor")
    stream_mid = (stream_in.astype(jnp.float32) + attended).astype(jnp.bfloat16)
    normal_mid = normed(stream_mid, gain_ffn)
    mid_mine = lax.dynamic_slice_in_dim(stream_mid, first_mine, rows_here, 0)
    gate_value = by_rows(normal_mid, gate_weight)
    up_value = by_rows(normal_mid, up_weight)
    hidden = (jax.nn.gelu(gate_value, approximate=True) * up_value).astype(jnp.bfloat16)
    ffn_result = lax.psum_scatter(
        jnp.dot(hidden, down_weight, preferred_element_type=jnp.float32),
        "tensor",
        scatter_dimension=0,
        tiled=True,
    )
    return (mid_mine.astype(jnp.float32) + ffn_result).astype(jnp.bfloat16)


Z, Y, C = 4, 2, 2
SPLIT = 4
PAD = 16
PIECES = 2
MESH = pl.DeviceIdType.MESH


def fits(mesh):
    return mesh.shape["tensor"] == Z * Y * C


def fused_kernel(
    payload, wq, wk, wv, wo, wg, wu, wd, src_ref, pair_rows, pair_cols, gain1, gain2,
    out_ref,
    arrived, stream, normal, wqkv_v, wo_v, wg_v, wu_v, wd_v, ctx, hid, mid, gathered,
    part1, rcore1, s1a, ry1, s2a, rz1, part2, rcore2, s1b, ry2, s2b, rz2,
    acc, summed, wsem, ag1_s, ag1_r, ag2_s, ag2_r, rs1_s, rs1_r, rs2_s, rs2_r,
):
    me = lax.axis_index("tensor")
    z, y, c = me // (Y * C), (me // C) % Y, me % C

    def flat(zi, yi, ci):
        return zi * (Y * C) + yi * C + ci

    ypart = flat(z, 1 - y, c)
    cpart = flat(z, y, 1 - c)

    own = pltpu.make_async_copy(payload, arrived.at[me], wsem.at[0])
    own.start()
    loads = [
        pltpu.make_async_copy(src, dst, wsem.at[1 + i])
        for i, (src, dst) in enumerate(
            [
                (wq, wqkv_v.at[pl.ds(0, HDIM)]),
                (wk, wqkv_v.at[pl.ds(HDIM, HDIM)]),
                (wv, wqkv_v.at[pl.ds(2 * HDIM, HDIM)]),
                (wo, wo_v),
                (wg, wg_v),
                (wu, wu_v),
                (wd, wd_v),
            ]
        )
    ]
    for load in loads:
        load.start()

    barrier = pltpu.get_barrier_semaphore()
    def greet(peer):
        pl.semaphore_signal(barrier, inc=1, device_id={"tensor": peer}, device_id_type=MESH)

    greet(ypart)
    greet(cpart)
    pl.when(z > 0)(lambda: greet(flat(z - 1, y, c)))
    pl.when(z + 1 < Z)(lambda: greet(flat(z + 1, y, c)))
    pl.semaphore_wait(barrier, jnp.where((z == 0) | (z + 1 == Z), 3, 4))

    def remote(src, dst, ssem, rsem, peer):
        return pltpu.make_async_remote_copy(
            src_ref=src, dst_ref=dst, send_sem=ssem, recv_sem=rsem,
            device_id={"tensor": peer}, device_id_type=MESH,
        )

    def gather(buf, ss, rs):
        lsem, ysem, csem = Z - 1, 2 * Z - 2, 3 * Z - 2

        count = 3 * Z - 2 + Z * Y
        size = buf.shape[1] // PIECES

        def move(p, idx, sem, peer):
            piece = buf.at[idx, pl.ds(p * size, size)]
            at = p * count + sem
            return remote(piece, piece, ss.at[at], rs.at[at], peer)

        def right(p, s):
            return move(p, flat(z - s, y, c), s, flat(z + 1, y, c))

        def left(p, s):
            return move(p, flat(z + s, y, c), lsem + s, flat(z - 1, y, c))

        def row(p, zi):
            return move(p, flat(zi, y, c), ysem + zi, ypart)

        def core(p, zi, yi):
            return move(p, flat(zi, yi, c), csem + zi * Y + yi, cpart)

        def fan(p, zi):
            row(p, zi).start()
            core(p, zi, y).start()

        def from_row(p, zi):
            move(p, flat(zi, 1 - y, c), ysem + zi, ypart).wait_recv()
            core(p, zi, 1 - y).start()

        for p in range(PIECES):
            pl.when(z + 1 < Z)(lambda: right(p, 0).start())
            pl.when(z > 0)(lambda: left(p, 0).start())
            fan(p, z)
        for s in range(Z - 1):
            for p in range(PIECES):

                @pl.when(z - 1 - s >= 0)
                def _():
                    zi = z - 1 - s
                    move(p, flat(zi, y, c), s, flat(z - 1, y, c)).wait_recv()
                    if s + 1 < Z - 1:
                        pl.when(z + 1 < Z)(lambda: right(p, s + 1).start())
                    fan(p, zi)

                @pl.when(z + 1 + s < Z)
                def _():
                    zi = z + 1 + s
                    move(p, flat(zi, y, c), lsem + s, flat(z + 1, y, c)).wait_recv()
                    if s + 1 < Z - 1:
                        pl.when(z > 0)(lambda: left(p, s + 1).start())
                    fan(p, zi)

        for s in range(Z):
            for p in range(PIECES):
                pl.when(z - s >= 0)(lambda: from_row(p, z - s))
                if s:
                    pl.when(z + s < Z)(lambda: from_row(p, z + s))
        for p in range(PIECES):
            for zi in range(Z):
                for yi in range(Y):
                    idx = flat(zi, yi, 1 - c)
                    move(p, idx, csem + zi * Y + yi, cpart).wait_recv()

        def drain():
            for p in range(PIECES):
                for s in range(Z - 1):
                    pl.when((z - s >= 0) & (z + 1 < Z))(lambda: right(p, s).wait_send())
                    pl.when((z + s < Z) & (z > 0))(lambda: left(p, s).wait_send())
                for zi in range(Z):
                    row(p, zi).wait_send()
                    for yi in range(Y):
                        core(p, zi, yi).wait_send()

        return drain

    def scatter_sum(left, weight, part, rcore, s1, ry, s2, rz, ss, rs):
        features = weight.shape[1]
        tile = features // 4

        def place(i):
            return jnp.where(z < Z // 2, Z - 1 - i, i)

        def core_copy(zi):
            return remote(part.at[zi, 1 - c], rcore.at[zi], ss.at[zi], rs.at[zi], cpart)

        def row_copy(zi):
            return remote(s1.at[zi], ry.at[zi], ss.at[Z + zi], rs.at[Z + zi], ypart)

        def right_copy(zi, peer):
            sem = 2 * Z + zi
            return remote(s2.at[zi], rz.at[zi], ss.at[sem], rs.at[sem], flat(peer, y, c))

        def left_copy(zi, peer):
            sem = 3 * Z + zi
            return remote(s2.at[zi], rz.at[Z + zi], ss.at[sem], rs.at[sem], flat(peer, y, c))

        def f32(v):
            return v.astype(jnp.float32)

        def one(i, carry):
            zi = place(i)
            rows = left[zi]
            for t in range(4):
                cols = pl.ds(t * tile, tile)
                found = jnp.dot(rows, weight[:, cols], preferred_element_type=jnp.float32)
                for yi in range(Y):
                    for ci in range(C):
                        at = (yi * C + ci) * PAD
                        part[zi, ci, yi, :, cols] = found[at : at + PAD].astype(jnp.bfloat16)
            core_copy(zi).start()
            return carry

        lax.fori_loop(0, Z, one, 0)

        def two(i, carry):
            zi = place(i)
            core_copy(zi).wait_recv()
            s1[zi] = (f32(part[zi, c, 1 - y]) + f32(rcore[zi, 1 - y])).astype(jnp.bfloat16)
            row_copy(zi).start()
            return carry

        lax.fori_loop(0, Z, two, 0)

        def three(i, carry):
            zi = place(i)
            row_copy(zi).wait_recv()
            acc[...] = f32(part[zi, c, y]) + f32(rcore[zi, y]) + f32(ry[zi])

            @pl.when((zi > z) & (z > 0))
            def _():
                right_copy(zi, z - 1).wait_recv()
                acc[...] += f32(rz[zi])

            @pl.when((zi < z) & (z + 1 < Z))
            def _():
                left_copy(zi, z + 1).wait_recv()
                acc[...] += f32(rz[Z + zi])

            @pl.when(zi > z)
            def _():
                s2[zi] = acc[...].astype(jnp.bfloat16)
                right_copy(zi, z + 1).start()

            @pl.when(zi < z)
            def _():
                s2[zi] = acc[...].astype(jnp.bfloat16)
                left_copy(zi, z - 1).start()

            @pl.when(zi == z)
            def _():
                summed[...] = acc[...]

            return carry

        lax.fori_loop(0, Z, three, 0)

        @pl.when(z > 0)
        def _():
            right_copy(z, z - 1).wait_recv()
            summed[...] += f32(rz[z])

        @pl.when(z + 1 < Z)
        def _():
            left_copy(z, z + 1).wait_recv()
            summed[...] += f32(rz[Z + z])

        for zi in range(Z):
            core_copy(zi).wait_send()
            row_copy(zi).wait_send()
            pl.when(zi > z)(lambda: right_copy(zi, z + 1).wait_send())
            pl.when(zi < z)(lambda: left_copy(zi, z - 1).wait_send())
        return summed[...]

    own.wait()
    drain = gather(arrived, ag1_s, ag1_r)
    slots, features = arrived.shape[0] * arrived.shape[1], stream.shape[1]
    tokens = stream.shape[0]
    width = features // SPLIT
    per = arrived.shape[1] // SPLIT
    spot = lax.broadcasted_iota(jnp.int32, (tokens, slots), 1)
    for j in range(SPLIT):
        chosen = (spot == src_ref[...] + j * per).astype(jnp.float32).astype(jnp.bfloat16)
        stream[:, pl.ds(j * width, width)] = jnp.dot(
            chosen, arrived[...].reshape(slots, width), preferred_element_type=jnp.float32
        ).astype(jnp.bfloat16)

    def norm_rows(i, carry):
        at = pl.ds(pl.multiple_of(i * PAD, PAD), PAD)
        normal[at, :] = normed(stream[at, :], gain1[...])
        return carry

    lax.fori_loop(0, tokens // PAD, norm_rows, 0)
    for load in loads[:4]:
        load.wait()
    qkv = by_rows(normal[...], wqkv_v[...]).astype(jnp.bfloat16)
    q, k, v = qkv[:, :HDIM], qkv[:, HDIM : 2 * HDIM], qkv[:, 2 * HDIM :]
    scores = by_rows(q, k) * HDIM ** (-0.5)
    scores = jnp.where(pair_rows[...] == pair_cols[...], scores, -1e30)
    weights = jnp.exp(scores - jnp.max(scores, axis=-1, keepdims=True))
    probability = (weights / jnp.sum(weights, axis=-1, keepdims=True)).astype(jnp.bfloat16)
    context = jnp.dot(probability, v, preferred_element_type=jnp.float32).astype(jnp.bfloat16)
    ctx[...] = context.reshape(ctx.shape)
    drain()

    total = scatter_sum(ctx, wo_v, part1, rcore1, s1a, ry1, s2a, rz1, rs1_s, rs1_r)
    mine = stream[pl.ds(pl.multiple_of(me * PAD, PAD), PAD), :]
    mid[...] = (mine.astype(jnp.float32) + total).astype(jnp.bfloat16)
    gathered[me] = normed(mid[...], gain2[...])
    drain = gather(gathered, ag2_s, ag2_r)
    for load in loads[4:]:
        load.wait()
    rows = gathered[...].reshape(tokens, features)
    gate_value = by_rows(rows, wg_v[...])
    up_value = by_rows(rows, wu_v[...])
    hidden = (jax.nn.gelu(gate_value, approximate=True) * up_value).astype(jnp.bfloat16)
    hid[...] = hidden.reshape(hid.shape)
    drain()
    total = scatter_sum(hid, wd_v, part2, rcore2, s1b, ry2, s2b, rz2, rs2_s, rs2_r)
    out_ref[...] = (mid[...].astype(jnp.float32) + total)[: out_ref.shape[0]].astype(jnp.bfloat16)


def fused_body(
    queries, corpus, block_owner, slot_row, segment, query_weight, key_weight, value_weight,
    out_weight, gain_attn, gain_ffn, gate_weight, up_weight, down_weight,
):
    n = lax.axis_size("tensor")
    my_index = lax.axis_index("tensor")
    owners = block_owner[:, 0]
    blocks = owners.shape[0]
    query_rows, features = queries.shape
    per = query_rows + CAP * BLK
    tokens = n * query_rows + blocks * BLK
    rows_here = tokens // n
    positions = jnp.arange(blocks, dtype=jnp.int32)
    earlier = (owners[:, None] == owners[None, :]) & (positions[:, None] < positions[None, :])
    slot_rank = jnp.sum(earlier.astype(jnp.int32), axis=0)
    slot_ids = jnp.arange(CAP, dtype=jnp.int32)
    choose_slot = (owners[None, :] == my_index) & (slot_rank[None, :] == slot_ids[:, None])
    local_rows = jnp.sum(jnp.where(choose_slot, slot_row[None, :], 0), axis=1)
    outgoing = jnp.take(corpus, local_rows, axis=0).reshape(CAP * BLK, features)
    width = features // SPLIT
    payload = (
        jnp.concatenate([queries, outgoing], axis=0)
        .reshape(per, SPLIT, width)
        .transpose(1, 0, 2)
        .reshape(SPLIT * per, width)
    )
    query_ids = jnp.arange(n * query_rows, dtype=jnp.int32)
    starts = owners * (SPLIT * per) + query_rows + slot_rank * BLK
    token_ids = jnp.arange(BLK, dtype=jnp.int32)
    source = jnp.concatenate(
        [
            query_ids // query_rows * (SPLIT * per) + query_ids % query_rows,
            (starts[:, None] + token_ids[None, :]).reshape(-1),
        ]
    )
    pair = jnp.concatenate([query_ids // QLEN, jnp.repeat(segment, BLK)])

    def padded(v, fill):
        return jnp.pad(
            v.reshape(n, rows_here), ((0, 0), (0, PAD - rows_here)), constant_values=fill
        ).reshape(-1)

    source = padded(source, -(2**20))
    pair = padded(pair, -1)
    rows = n * PAD
    hidden = gate_weight.shape[0]
    bf = jnp.bfloat16
    chunk = (PAD, features)
    scatter_bufs = [
        pltpu.VMEM((Z, C, Y) + chunk, bf),
        pltpu.VMEM((Z, Y) + chunk, bf),
        pltpu.VMEM((Z,) + chunk, bf),
        pltpu.VMEM((Z,) + chunk, bf),
        pltpu.VMEM((Z,) + chunk, bf),
        pltpu.VMEM((2 * Z,) + chunk, bf),
    ]
    dma = pltpu.SemaphoreType.DMA
    gather_sems = (PIECES * (3 * Z - 2 + Z * Y),)
    scatter_sems = (4 * Z,)
    any_spec = pl.BlockSpec(memory_space=pl.ANY)
    vmem_spec = pl.BlockSpec(memory_space=pltpu.VMEM)
    return pl.pallas_call(
        fused_kernel,
        out_shape=jax.ShapeDtypeStruct((rows_here, features), bf),
        in_specs=[any_spec] * 8 + [vmem_spec] * 5,
        out_specs=vmem_spec,
        scratch_shapes=[
            pltpu.VMEM((n, SPLIT * per, width), bf),
            pltpu.VMEM((rows, features), bf),
            pltpu.VMEM((rows, features), bf),
            pltpu.VMEM((3 * HDIM, features), bf),
            pltpu.VMEM((HDIM, features), bf),
            pltpu.VMEM((hidden, features), bf),
            pltpu.VMEM((hidden, features), bf),
            pltpu.VMEM((hidden, features), bf),
            pltpu.VMEM((Z, rows // Z, HDIM), bf),
            pltpu.VMEM((Z, rows // Z, hidden), bf),
            pltpu.VMEM(chunk, bf),
            pltpu.VMEM((n,) + chunk, bf),
        ]
        + scatter_bufs
        + scatter_bufs
        + [pltpu.VMEM(chunk, jnp.float32)] * 2
        + [dma((8,))]
        + [dma(gather_sems)] * 4
        + [dma(scatter_sems)] * 4,
        compiler_params=pltpu.CompilerParams(
            collective_id=0, has_side_effects=True, vmem_limit_bytes=56 * 2**20
        ),
    )(
        payload, query_weight, key_weight, value_weight, out_weight, gate_weight, up_weight,
        down_weight, source[:, None], pair[:, None], pair[None, :],
        gain_attn[None, :], gain_ffn[None, :],
    )


def solution(mesh):
    placed = (
        P(("groups", "tensor"), None),
        P(("groups", "tensor"), None, None),
        P("groups", None),
        P("groups"),
        P("groups"),
        P("tensor", None),
        P("tensor", None),
        P("tensor", None),
        P("tensor", None),
        P(),
        P(),
        P("tensor", None),
        P("tensor", None),
        P("tensor", None),
    )
    body = fused_body if fits(mesh) else plain_body
    return jax.shard_map(
        body, mesh=mesh, in_specs=placed, out_specs=P(("groups", "tensor"), None), check_vma=False
    )
```
